32 devices in a mesh: dp: 8 (over y, x, core), seq: 4 (over z).
Axes of the slice: x: 2, y: 2, z: 4, core: 2. Of those that a mesh axis runs over, the one named last changes fastest.
Arguments:
- query: bfloat16 [8, 512, 512], P('dp', 'seq'), may hold values from -8 to 8
- key: bfloat16 [8, 512, 512], P('dp', 'seq'), may hold values from -8 to 8
- value: bfloat16 [8, 512, 512], P('dp', 'seq'), may hold values from -6 to 6
- out_ctx: bfloat16 [8, 512, 512], P('dp', 'seq'), may hold values from -6 to 6
- d_out: bfloat16 [8, 512, 512], P('dp', 'seq'), may hold values from -6 to 6
- score_bias: float32 [4, 4], P('seq'), may hold values from -2 to 2
- block_list: int32 [4, 4, 4], P('seq'), may hold values from 0 to 3, as said below
- block_count: int32 [4, 4], P('seq'), may hold values from 1 to 4, as said below
- hit_count: int32 [8], P('dp'), may hold values from 128 to 512, as said below
Outputs:
- d_query: bfloat16 [8, 512, 512], P('dp', 'seq')
- d_key: bfloat16 [8, 512, 512], P('dp', 'seq')
- d_value: bfloat16 [8, 512, 512], P('dp', 'seq')
- d_bias: float32 [4, 4], P('seq')
The draws below stay inside these ranges and needn't reach their ends.
Inputs may be any that keep to these rules, and one draw needn't show every extreme that they name: Each list block_list[h, q] holds 4 different key blocks, the first being block q itself; only its first block_count[h, q] entries are used. `block_count`: some head has a list with all 4 entries used. `hit_count`: some event has all 512 hits real.
All inputs are finite; a program needn't handle non-finite values.
Results may differ from the reference program's by a relative error of at most 0.0049.
Values may be sent and summed in bfloat16 or wider, within the bound.
A program may use at most 64 MiB of HBM per device.

```python
import math
import jax
import jax.numpy as jnp
from jax import lax

DH = 128
H = 4
D = 512
HITS = 512
EVENTS = 8
NKB = 4
KSLOTS = 4


def drawn_field(key):
    field = jax.random.truncated_normal(key, -6.0, 6.0, (EVENTS, HITS, D))
    return field.astype(jnp.float32)


def draw_query(key, part):
    field = drawn_field(jax.random.fold_in(key, 1))
    return field.astype(jnp.bfloat16)


def draw_key(key, part):
    field = drawn_field(jax.random.fold_in(key, 2))
    return field.astype(jnp.bfloat16)


def draw_hit_count(key, part):
    counts = jax.random.randint(key, (EVENTS,), HITS // 4, HITS + 1)
    fullest = jax.random.randint(jax.random.fold_in(key, 5), (), 0, EVENTS)
    return jnp.where(jnp.arange(EVENTS) == fullest, HITS, counts).astype(jnp.int32)


def draw_block_count(key, part):
    shifts = jax.random.randint(jax.random.fold_in(key, 1), (H,), 0, 4)
    busiest = jax.random.randint(jax.random.fold_in(key, 2), (), 0, H)
    shifts = jnp.where(jnp.arange(H) == busiest, 0, shifts)
    head_most = jnp.maximum(jnp.right_shift(jnp.full((H,), KSLOTS, jnp.int32), shifts), 1)
    raw = jax.random.randint(jax.random.fold_in(key, 3), (H, NKB), 0, 1 << 20)
    counts = 1 + raw % head_most[:, None]
    picked = jax.random.randint(jax.random.fold_in(key, 4), (H,), 0, NKB)
    counts = jnp.where(jnp.arange(NKB)[None, :] == picked[:, None], head_most[:, None], counts)
    return counts.astype(jnp.int32)


def draw_block_list(key, part):
    raw = jax.random.randint(key, (H, NKB, NKB), 0, 1 << 20)
    column = jnp.arange(NKB, dtype=jnp.int32)
    ranking = raw * NKB + column[None, None, :]
    ranking = jnp.where(column[None, :, None] == column[None, None, :], -1, ranking)
    ordered = jnp.argsort(ranking, axis=2, stable=True)
    return ordered[:, :, :KSLOTS].astype(jnp.int32)


def steps_of(rng, shape, cuts, low, top_value):
    level = 1.0
    for axis_at, blocks in cuts:
        steps = jax.random.uniform(jax.random.fold_in(jax.random.fold_in(rng, 6), axis_at), (blocks,), jnp.float32, low / len(cuts), top_value / len(cuts))
        level = level * jnp.repeat(jnp.exp(steps), shape[axis_at] // blocks).reshape((-1,) + (1,) * (len(shape) - 1 - axis_at))
    return level


def gaussian(key, extent, width, limit, split=(), kind=jnp.bfloat16):
    values = width * jax.random.normal(key, extent, jnp.float32)
    if split:
        values = values * steps_of(key, extent, split, -0.22, 0.18)
    return jnp.clip(values, -limit, limit).astype(kind)


def setup_inputs(seed: int = 0) -> dict:
    streams_of = jax.random.split(jax.random.key(seed), 10)
    query = draw_query(jax.random.fold_in(streams_of[9], 71), 0)
    key = draw_key(jax.random.fold_in(streams_of[9], 71), 0)
    value = gaussian(streams_of[2], (EVENTS, HITS, D), 1.0, 6.0, ((0, 8), (1, 4)))
    out_ctx = gaussian(streams_of[3], (EVENTS, HITS, D), 1.0, 6.0, ((0, 8), (1, 4)))
    d_out = gaussian(streams_of[4], (EVENTS, HITS, D), 1.0, 6.0, ((0, 8), (1, 4)))
    score_bias = jnp.clip(jax.random.uniform(streams_of[5], (H, NKB), jnp.float32, -2.0, 2.0) * steps_of(streams_of[5], (H, NKB), ((0, 4),), -0.4, 0.0), -2.0, 2.0)
    block_list = draw_block_list(jax.random.fold_in(streams_of[9], 71), 0)
    block_count = draw_block_count(jax.random.fold_in(streams_of[9], 71), 0)
    hit_count = draw_hit_count(jax.random.fold_in(streams_of[9], 71), 0)
    return {"query": query, "key": key, "value": value, "out_ctx": out_ctx, "d_out": d_out, "score_bias": score_bias, "block_list": block_list, "block_count": block_count, "hit_count": hit_count}


MASKED = -1000000000.0

def head_backward(query_head, key_head, value_head, grad_head, delta_head, bias_row, list_rows, count_row, hit_limit):
    nblocks, slots = list_rows.shape
    hits, head_dim = query_head.shape
    block = hits // nblocks
    scale = 1.0 / math.sqrt(head_dim)
    query_blocks = query_head.astype(jnp.float32).reshape(nblocks, block, head_dim)
    key_blocks = key_head.astype(jnp.float32).reshape(nblocks, block, head_dim)
    value_blocks = value_head.astype(jnp.float32).reshape(nblocks, block, head_dim)
    grad_blocks = grad_head.astype(jnp.float32).reshape(nblocks, block, head_dim)
    delta_blocks = delta_head.reshape(nblocks, block)
    within = jnp.arange(block, dtype=jnp.int32)
    row_valid = (jnp.arange(hits, dtype=jnp.int32) < hit_limit).reshape(nblocks, block)
    chosen = list_rows.T
    key_taken = key_blocks[chosen]
    value_taken = value_blocks[chosen]
    scores = jnp.einsum('qid,sqjd->sqij', query_blocks, key_taken) * scale + bias_row[chosen][:, :, None, None]
    slot_ids = jnp.arange(slots, dtype=jnp.int32)
    slot_used = (slot_ids[:, None] < count_row[None, :])[:, :, None, None]
    key_real = (chosen[:, :, None] * block + within[None, None, :] < hit_limit)[:, :, None, :]
    allowed = slot_used & key_real
    scores = jnp.where(allowed, scores, MASKED)
    row_top = lax.optimization_barrier(jnp.max(scores, axis=(0, 3)))
    row_total = lax.optimization_barrier(jnp.sum(jnp.exp(scores - row_top[None, :, :, None]), axis=(0, 3)))
    lse = row_top + jnp.log(row_total)
    probs = jnp.where(allowed & row_valid[None, :, :, None], jnp.exp(scores - lse[None, :, :, None]), 0.0)
    dprobs = jnp.einsum('qid,sqjd->sqij', grad_blocks, value_taken)
    dscores = probs * (dprobs - delta_blocks[None, :, :, None])
    probs_half = lax.optimization_barrier(probs.astype(jnp.bfloat16)).astype(jnp.float32)
    dscores_half = lax.optimization_barrier(dscores.astype(jnp.bfloat16)).astype(jnp.float32)
    d_query = jnp.einsum('sqij,sqjd->qid', dscores_half, key_taken) * scale
    key_terms = jnp.einsum('sqij,qid->sqjd', dscores_half, query_blocks)
    value_terms = jnp.einsum('sqij,qid->sqjd', probs_half, grad_blocks)
    flat = chosen.reshape(-1)
    d_key = jnp.zeros((nblocks, block, head_dim), jnp.float32).at[flat].add(key_terms.reshape(-1, block, head_dim)) * scale
    d_value = jnp.zeros((nblocks, block, head_dim), jnp.float32).at[flat].add(value_terms.reshape(-1, block, head_dim))
    d_bias = jnp.zeros((nblocks,), jnp.float32).at[flat].add(lax.optimization_barrier(jnp.sum(dscores, axis=(2, 3))).reshape(-1))
    return (d_query.reshape(hits, head_dim), d_key.reshape(hits, head_dim), d_value.reshape(hits, head_dim), d_bias)

def reference(query, key, value, out_ctx, d_out, score_bias, block_list, block_count, hit_count):

    def per_event(items):
        query_rows, key_rows, value_rows, out_rows, grad_rows, hit_limit = items
        row_valid = jnp.arange(HITS, dtype=jnp.int32) < hit_limit
        grad_kept = jnp.where(row_valid[:, None], grad_rows, jnp.zeros_like(grad_rows))

        def split_heads(field):
            return field.reshape(HITS, H, DH).transpose(1, 0, 2)
        delta = lax.optimization_barrier(jnp.sum(split_heads(grad_kept).astype(jnp.float32) * split_heads(out_rows).astype(jnp.float32), axis=2))
        grads = jax.vmap(head_backward, in_axes=(0, 0, 0, 0, 0, 0, 0, 0, None))(split_heads(query_rows), split_heads(key_rows), split_heads(value_rows), split_heads(grad_kept), delta, score_bias, block_list, block_count, hit_limit)

        def merge_heads(field):
            return field.transpose(1, 0, 2).reshape(HITS, D).astype(jnp.bfloat16)
        return (merge_heads(grads[0]), merge_heads(grads[1]), merge_heads(grads[2]), grads[3])
    d_query, d_key, d_value, bias_terms = lax.map(per_event, (query, key, value, out_ctx, d_out, hit_count))
    return (d_query, d_key, d_value, lax.optimization_barrier(jnp.sum(bias_terms, axis=0)))
```

```python
import functools
import math

import jax
import jax.numpy as jnp
from jax import lax
from jax.experimental import pallas as pl
from jax.experimental.pallas import tpu as pltpu
from jax.sharding import PartitionSpec as P

MASKED = -1000000000.0
MESH = pl.DeviceIdType.MESH
KEY, QUERY, GRAD, VALUE, DELTA, DVALUE, DKEY, DQUERY = range(8)


def kernel(
    n,
    ndp,
    head_dim,
    q_hbm,
    k_hbm,
    v_hbm,
    o_hbm,
    g_hbm,
    bias_ref,
    list_ref,
    count_ref,
    hit_ref,
    dq_hbm,
    dk_hbm,
    dv_hbm,
    db_ref,
    kbuf,
    qbuf,
    gbuf,
    vbuf,
    delta_in,
    delta_out,
    g_own,
    o_own,
    probs,
    probs_half,
    ds_half,
    dv_out,
    dk_out,
    dq_out,
    bias_out,
    bias_in,
    send_sem,
    recv_sem,
    own_sem,
    bias_send,
    bias_recv,
):
    me = lax.axis_index("seq")
    here = lax.axis_index("dp")
    rows = q_hbm.shape[1]
    hits = n * rows
    slots = list_ref.shape[2]
    scale = 1.0 / math.sqrt(head_dim)
    above = n - 1 - me

    def peer_of(r):
        return jnp.where(r < above, n - 1 - r, r - above)

    def source_of(r):
        return me if r == 0 else peer_of(n - 1 - r)

    def lanes(h):
        return pl.ds(pl.multiple_of(h * head_dim, head_dim), head_dim)

    load_g = pltpu.make_async_copy(g_hbm.at[0], g_own, own_sem.at[DVALUE])
    load_o = pltpu.make_async_copy(o_hbm.at[0], o_own, own_sem.at[DKEY])
    load_g.start()
    load_o.start()
    sources = {KEY: k_hbm, QUERY: q_hbm, GRAD: g_hbm, VALUE: v_hbm}
    targets = {KEY: kbuf, QUERY: qbuf, GRAD: gbuf, VALUE: vbuf}
    own = {}
    for kind in (KEY, QUERY, GRAD, VALUE):
        own[kind] = pltpu.make_async_copy(
            sources[kind].at[0, :, lanes(me)], targets[kind].at[me], own_sem.at[kind]
        )
        own[kind].start()

    barrier = pltpu.get_barrier_semaphore()
    for r in range(n - 1):
        pl.semaphore_signal(barrier, inc=1, device_id={"seq": peer_of(r)}, device_id_type=MESH)
    for r in range(1, ndp):
        pl.semaphore_signal(
            barrier, inc=1, device_id={"dp": lax.rem(here + r, ndp)}, device_id_type=MESH
        )
    pl.semaphore_wait(barrier, n - 1 + ndp - 1)

    def out_copy(kind, peer):
        return pltpu.make_async_remote_copy(
            src_ref=sources[kind].at[0, :, lanes(peer)],
            dst_ref=targets[kind].at[me],
            send_sem=send_sem.at[kind, peer],
            recv_sem=recv_sem.at[kind, me],
            device_id={"seq": peer},
            device_id_type=MESH,
        )

    def wait_in(kind, buf, peer):
        pltpu.make_async_remote_copy(
            src_ref=buf,
            dst_ref=buf,
            send_sem=send_sem.at[kind, peer],
            recv_sem=recv_sem.at[kind, peer],
            device_id={"seq": peer},
            device_id_type=MESH,
        ).wait_recv()

    sent = []

    def send(copy):
        copy.start()
        sent.append(copy)

    for kind in (KEY, QUERY):
        for r in range(n - 1):
            send(out_copy(kind, peer_of(r)))

    load_g.wait()
    load_o.wait()
    for h in range(n):
        cols = slice(h * head_dim, (h + 1) * head_dim)
        product = g_own[:, cols].astype(jnp.float32) * o_own[:, cols].astype(jnp.float32)
        delta_out[h] = jnp.sum(product.T, axis=0, keepdims=True)
    for r in range(n - 1):
        peer = peer_of(r)
        send(
            pltpu.make_async_remote_copy(
                src_ref=delta_out.at[peer],
                dst_ref=delta_in.at[me],
                send_sem=send_sem.at[DELTA, peer],
                recv_sem=recv_sem.at[DELTA, me],
                device_id={"seq": peer},
                device_id_type=MESH,
            )
        )
    delta_in[me] = delta_out[me]
    for kind in (GRAD, VALUE):
        for r in range(n - 1):
            send(out_copy(kind, peer_of(r)))

    hit_limit = hit_ref[0]
    for kind in (KEY, QUERY):
        own[kind].wait()
        for r in range(n - 1):
            peer = peer_of(r)
            wait_in(kind, targets[kind].at[peer], peer)
    q_all = qbuf[...].reshape(hits, head_dim)
    lane = lax.broadcasted_iota(jnp.int32, (1, hits), 1)
    within = lax.broadcasted_iota(jnp.int32, (rows, 1), 0)

    def score_step(b, top):
        shift = jnp.full((1, hits), MASKED, jnp.float32)
        for qb in range(n):
            used = jnp.int32(0)
            for s in range(slots):
                hit = (list_ref[0, qb, s] == b) & (s < count_ref[0, qb])
                used = jnp.where(hit, jnp.int32(1), used)
            inside = (lane >= qb * rows) & (lane < (qb + 1) * rows)
            shift = jnp.where(inside & (used > 0), bias_ref[0, b], shift)
        real = jnp.where(b * rows + within < hit_limit, 0.0, MASKED)
        scores = (
            lax.dot_general(
                kbuf[b], q_all, (((1,), (1,)), ((), ())), preferred_element_type=jnp.float32
            )
            * scale
        )
        scores = (scores + shift) + real
        probs[b] = scores
        return jnp.maximum(top, jnp.max(scores, axis=0, keepdims=True))

    short = n <= 4
    top = lax.fori_loop(
        0, n, score_step, jnp.full((1, hits), -3e9, jnp.float32), unroll=short
    )

    def exp_step(b, total):
        raised = jnp.exp(probs[b] - top)
        probs[b] = raised
        return total + jnp.sum(raised, axis=0, keepdims=True)

    total = lax.fori_loop(0, n, exp_step, jnp.zeros((1, hits), jnp.float32), unroll=short)
    factor = jnp.where(lane < hit_limit, 1.0 / total, 0.0)

    def scale_step(b, carry):
        scaled = probs[b] * factor
        probs[b] = scaled
        probs_half[b] = scaled.astype(jnp.bfloat16)
        return carry

    lax.fori_loop(0, n, scale_step, 0, unroll=short)

    def back_copy(kind, buf, out, peer):
        return pltpu.make_async_remote_copy(
            src_ref=buf.at[peer],
            dst_ref=out.at[0, :, lanes(me)],
            send_sem=send_sem.at[kind, peer],
            recv_sem=recv_sem.at[kind, me],
            device_id={"seq": peer},
            device_id_type=MESH,
        )

    def keep_copy(kind, buf, out):
        copy = pltpu.make_async_copy(buf.at[me], out.at[0, :, lanes(me)], own_sem.at[kind])
        copy.start()
        return copy

    kept = []
    own[GRAD].wait()
    for r in range(n - 1):
        peer = peer_of(r)
        wait_in(GRAD, gbuf.at[peer], peer)
    g_all = gbuf[...].reshape(hits, head_dim)
    for r in range(n):
        b = peer_of(r) if r < n - 1 else me
        dv_out[b] = jnp.dot(probs_half[b], g_all, preferred_element_type=jnp.float32).astype(
            jnp.bfloat16
        )
        if r < n - 1:
            send(back_copy(DVALUE, dv_out, dv_hbm, b))
        else:
            kept.append(keep_copy(DVALUE, dv_out, dv_hbm))

    for r in range(n - 1):
        peer = peer_of(r)
        wait_in(DELTA, delta_in.at[peer], peer)
    delta = jnp.concatenate([delta_in[b] for b in range(n)], axis=1)
    spot = lax.broadcasted_iota(jnp.int32, bias_out.shape, 1)
    bias_sums = jnp.zeros(bias_out.shape, jnp.float32)
    own[VALUE].wait()
    for r in range(n):
        b = source_of(r)
        if r > 0:
            wait_in(VALUE, vbuf.at[b], b)
        dprobs = lax.dot_general(
            vbuf[b], g_all, (((1,), (1,)), ((), ())), preferred_element_type=jnp.float32
        )
        dscores = probs[b] * (dprobs - delta)
        half = dscores.astype(jnp.bfloat16)
        ds_half[b] = half
        grad = jnp.dot(half, q_all, preferred_element_type=jnp.float32)
        dk_out[b] = (grad * scale).astype(jnp.bfloat16)
        if r > 0:
            send(back_copy(DKEY, dk_out, dk_hbm, b))
        else:
            kept.append(keep_copy(DKEY, dk_out, dk_hbm))
        block_sum = jnp.sum(jnp.sum(dscores, axis=0, keepdims=True), axis=1, keepdims=True)
        bias_sums = bias_sums + jnp.where(spot == b, block_sum, 0.0)
    bias_out[...] = bias_sums
    bias_sent = []
    for r in range(1, ndp):
        copy = pltpu.make_async_remote_copy(
            src_ref=bias_out,
            dst_ref=bias_in.at[here],
            send_sem=bias_send.at[r],
            recv_sem=bias_recv.at[here],
            device_id={"dp": lax.rem(here + r, ndp)},
            device_id_type=MESH,
        )
        copy.start()
        bias_sent.append(copy)
    bias_in[here] = bias_sums

    k_all = kbuf[...].reshape(hits, head_dim)
    for r in range(n):
        b = peer_of(r) if r < n - 1 else me
        picked = ds_half[:, :, pl.ds(pl.multiple_of(b * rows, rows), rows)].reshape(hits, rows)
        grad = lax.dot_general(
            picked, k_all, (((0,), (0,)), ((), ())), preferred_element_type=jnp.float32
        )
        dq_out[b] = (grad * scale).astype(jnp.bfloat16)
        if r < n - 1:
            send(back_copy(DQUERY, dq_out, dq_hbm, b))
        else:
            kept.append(keep_copy(DQUERY, dq_out, dq_hbm))

    for r in range(1, ndp):
        other = lax.rem(here + r, ndp)
        pltpu.make_async_remote_copy(
            src_ref=bias_in.at[other],
            dst_ref=bias_in.at[other],
            send_sem=bias_send.at[r],
            recv_sem=bias_recv.at[other],
            device_id={"dp": other},
            device_id_type=MESH,
        ).wait_recv()
    db_ref[...] = jnp.sum(bias_in[...], axis=0)[:, : db_ref.shape[1]]

    for kind, out in ((DVALUE, dv_hbm), (DKEY, dk_hbm), (DQUERY, dq_hbm)):
        for r in range(n - 1):
            peer = peer_of(r)
            wait_in(kind, out.at[0, :, lanes(peer)], peer)
    for copy in sent + bias_sent:
        copy.wait_send()
    for copy in kept:
        copy.wait()


def on_device(query, key, value, out_ctx, d_out, score_bias, block_list, block_count, hit_count):
    n = lax.axis_size("seq")
    ndp = lax.axis_size("dp")
    _, rows, width = query.shape
    head_dim = width // (score_bias.shape[0] * n)
    assert score_bias.shape[0] == 1 and block_list.shape[1] == n
    hits = n * rows
    padded = -(-n // 128) * 128
    half, full = jnp.bfloat16, jnp.float32
    any_ref = pl.BlockSpec(memory_space=pl.ANY)
    smem = pl.BlockSpec(memory_space=pltpu.SMEM)
    field = jax.ShapeDtypeStruct(query.shape, query.dtype)
    return pl.pallas_call(
        functools.partial(kernel, n, ndp, head_dim),
        out_shape=(field, field, field, jax.ShapeDtypeStruct((1, n), full)),
        in_specs=[any_ref] * 5 + [smem] * 4,
        out_specs=(any_ref, any_ref, any_ref, pl.BlockSpec(memory_space=pltpu.VMEM)),
        scratch_shapes=[
            pltpu.VMEM((n, rows, head_dim), half),
            pltpu.VMEM((n, rows, head_dim), half),
            pltpu.VMEM((n, rows, head_dim), half),
            pltpu.VMEM((n, rows, head_dim), half),
            pltpu.VMEM((n, 1, rows), full),
            pltpu.VMEM((n, 1, rows), full),
            pltpu.VMEM((rows, width), half),
            pltpu.VMEM((rows, width), half),
            pltpu.VMEM((n, rows, hits), full),
            pltpu.VMEM((n, rows, hits), half),
            pltpu.VMEM((n, rows, hits), half),
            pltpu.VMEM((n, rows, head_dim), half),
            pltpu.VMEM((n, rows, head_dim), half),
            pltpu.VMEM((n, rows, head_dim), half),
            pltpu.VMEM((1, padded), full),
            pltpu.VMEM((ndp, 1, padded), full),
            pltpu.SemaphoreType.DMA((8, n)),
            pltpu.SemaphoreType.DMA((8, n)),
            pltpu.SemaphoreType.DMA((8,)),
            pltpu.SemaphoreType.DMA((ndp,)),
            pltpu.SemaphoreType.DMA((ndp,)),
        ],
        compiler_params=pltpu.CompilerParams(
            collective_id=0, has_side_effects=True, vmem_limit_bytes=60 * 1024 * 1024
        ),
    )(query, key, value, out_ctx, d_out, score_bias, block_list, block_count, hit_count)


def solution(mesh):
    placed = (
        P("dp", "seq", None),
        P("dp", "seq", None),
        P("dp", "seq", None),
        P("dp", "seq", None),
        P("dp", "seq", None),
        P("seq", None),
        P("seq", None, None),
        P("seq", None),
        P("dp"),
    )
    return jax.shard_map(
        on_device,
        mesh=mesh,
        in_specs=placed,
        out_specs=(
            P("dp", "seq", None),
            P("dp", "seq", None),
            P("dp", "seq", None),
            P("seq", None),
        ),
        check_vma=False,
    )
```

```python
import functools
import math

import jax
import jax.numpy as jnp
from jax import lax
from jax.experimental import pallas as pl
from jax.experimental.pallas import tpu as pltpu
from jax.sharding import PartitionSpec as P

MASKED = -1000000000.0
MESH = pl.DeviceIdType.MESH
KEY, QUERY, GRAD, VALUE, DELTA, DVALUE, DKEY, DQUERY = range(8)


def kernel(
    n,
    ndp,
    head_dim,
    q_hbm,
    k_hbm,
    v_hbm,
    o_hbm,
    g_hbm,
    bias_hbm,
    list_hbm,
    count_hbm,
    hit_hbm,
    dq_ref,
    dk_ref,
    dv_ref,
    db_ref,
    kbuf,
    qbuf,
    gbuf,
    vbuf,
    delta_in,
    delta_out,
    g_own,
    o_own,
    probs,
    probs_half,
    ds_half,
    dv_out,
    dk_out,
    dq_out,
    bias_out,
    bias_in,
    bias_ref,
    list_ref,
    count_ref,
    hit_ref,
    send_sem,
    recv_sem,
    own_sem,
    bias_send,
    bias_recv,
    table_sem,
):
    me = lax.axis_index("seq")
    here = lax.axis_index("dp")
    rows = q_hbm.shape[1]
    hits = n * rows
    slots = list_ref.shape[2]
    scale = 1.0 / math.sqrt(head_dim)
    above = n - 1 - me

    def peer_of(r):
        return jnp.where(r < above, n - 1 - r, r - above)

    def source_of(r):
        return me if r == 0 else peer_of(n - 1 - r)

    def lanes(h):
        return pl.ds(pl.multiple_of(h * head_dim, head_dim), head_dim)

    load_g = pltpu.make_async_copy(g_hbm.at[0], g_own, own_sem.at[DVALUE])
    load_o = pltpu.make_async_copy(o_hbm.at[0], o_own, own_sem.at[DKEY])
    load_g.start()
    load_o.start()
    tables = [
        pltpu.make_async_copy(src, dst, table_sem.at[i])
        for i, (src, dst) in enumerate(
            ((bias_hbm, bias_ref), (list_hbm, list_ref), (count_hbm, count_ref), (hit_hbm, hit_ref))
        )
    ]
    for copy in tables:
        copy.start()
    sources = {KEY: k_hbm, QUERY: q_hbm, GRAD: g_hbm, VALUE: v_hbm}
    targets = {KEY: kbuf, QUERY: qbuf, GRAD: gbuf, VALUE: vbuf}
    own = {}
    for kind in (KEY, QUERY, GRAD, VALUE):
        own[kind] = pltpu.make_async_copy(
            sources[kind].at[0, :, lanes(me)], targets[kind].at[me], own_sem.at[kind]
        )
        own[kind].start()

    barrier = pltpu.get_barrier_semaphore()
    for r in range(n - 1):
        pl.semaphore_signal(barrier, inc=1, device_id={"seq": peer_of(r)}, device_id_type=MESH)
    for r in range(1, ndp):
        pl.semaphore_signal(
            barrier, inc=1, device_id={"dp": lax.rem(here + r, ndp)}, device_id_type=MESH
        )
    pl.semaphore_wait(barrier, n - 1 + ndp - 1)

    def out_copy(kind, peer):
        return pltpu.make_async_remote_copy(
            src_ref=sources[kind].at[0, :, lanes(peer)],
            dst_ref=targets[kind].at[me],
            send_sem=send_sem.at[kind, peer],
            recv_sem=recv_sem.at[kind, me],
            device_id={"seq": peer},
            device_id_type=MESH,
        )

    def wait_in(kind, buf, peer):
        pltpu.make_async_remote_copy(
            src_ref=buf,
            dst_ref=buf,
            send_sem=send_sem.at[kind, peer],
            recv_sem=recv_sem.at[kind, peer],
            device_id={"seq": peer},
            device_id_type=MESH,
        ).wait_recv()

    sent = []

    def send(copy):
        copy.start()
        sent.append(copy)

    for kind in (KEY, QUERY):
        for r in range(n - 1):
            send(out_copy(kind, peer_of(r)))

    load_g.wait()
    load_o.wait()
    for h in range(n):
        cols = slice(h * head_dim, (h + 1) * head_dim)
        product = g_own[:, cols].astype(jnp.float32) * o_own[:, cols].astype(jnp.float32)
        delta_out[h] = jnp.sum(product.T, axis=0, keepdims=True)
    for r in range(n - 1):
        peer = peer_of(r)
        send(
            pltpu.make_async_remote_copy(
                src_ref=delta_out.at[peer],
                dst_ref=delta_in.at[me],
                send_sem=send_sem.at[DELTA, peer],
                recv_sem=recv_sem.at[DELTA, me],
                device_id={"seq": peer},
                device_id_type=MESH,
            )
        )
    delta_in[me] = delta_out[me]
    for kind in (GRAD, VALUE):
        for r in range(n - 1):
            send(out_copy(kind, peer_of(r)))

    for copy in tables:
        copy.wait()
    hit_limit = hit_ref[0]
    for kind in (KEY, QUERY):
        own[kind].wait()
        for r in range(n - 1):
            peer = peer_of(r)
            wait_in(kind, targets[kind].at[peer], peer)
    q_all = qbuf[...].reshape(hits, head_dim)
    lane = lax.broadcasted_iota(jnp.int32, (1, hits), 1)
    within = lax.broadcasted_iota(jnp.int32, (rows, 1), 0)

    def score_step(b, top):
        shift = jnp.full((1, hits), MASKED, jnp.float32)
        for qb in range(n):
            used = jnp.int32(0)
            for s in range(slots):
                hit = (list_ref[0, qb, s] == b) & (s < count_ref[0, qb])
                used = jnp.where(hit, jnp.int32(1), used)
            inside = (lane >= qb * rows) & (lane < (qb + 1) * rows)
            shift = jnp.where(inside & (used > 0), bias_ref[0, b], shift)
        real = jnp.where(b * rows + within < hit_limit, 0.0, MASKED)
        scores = (
            lax.dot_general(
                kbuf[b], q_all, (((1,), (1,)), ((), ())), preferred_element_type=jnp.float32
            )
            * scale
        )
        scores = (scores + shift) + real
        probs[b] = scores
        return jnp.maximum(top, jnp.max(scores, axis=0, keepdims=True))

    short = n <= 4
    top = lax.fori_loop(
        0, n, score_step, jnp.full((1, hits), -3e9, jnp.float32), unroll=short
    )

    def exp_step(b, total):
        raised = jnp.exp(probs[b] - top)
        probs[b] = raised
        return total + jnp.sum(raised, axis=0, keepdims=True)

    total = lax.fori_loop(0, n, exp_step, jnp.zeros((1, hits), jnp.float32), unroll=short)
    factor = jnp.where(lane < hit_limit, 1.0 / total, 0.0)

    def scale_step(b, carry):
        scaled = probs[b] * factor
        probs[b] = scaled
        probs_half[b] = scaled.astype(jnp.bfloat16)
        return carry

    lax.fori_loop(0, n, scale_step, 0, unroll=short)

    def back_copy(kind, buf, out, peer):
        return pltpu.make_async_remote_copy(
            src_ref=buf.at[peer],
            dst_ref=out.at[:, lanes(me)],
            send_sem=send_sem.at[kind, peer],
            recv_sem=recv_sem.at[kind, me],
            device_id={"seq": peer},
            device_id_type=MESH,
        )

    own[GRAD].wait()
    for r in range(n - 1):
        peer = peer_of(r)
        wait_in(GRAD, gbuf.at[peer], peer)
    g_all = gbuf[...].reshape(hits, head_dim)
    for r in range(n):
        b = peer_of(r) if r < n - 1 else me
        grad = jnp.dot(probs_half[b], g_all, preferred_element_type=jnp.float32)
        if r < n - 1:
            dv_out[b] = grad.astype(jnp.bfloat16)
            send(back_copy(DVALUE, dv_out, dv_ref, b))
        else:
            dv_ref[:, lanes(me)] = grad.astype(jnp.bfloat16)

    for r in range(n - 1):
        peer = peer_of(r)
        wait_in(DELTA, delta_in.at[peer], peer)
    delta = jnp.concatenate([delta_in[b] for b in range(n)], axis=1)
    spot = lax.broadcasted_iota(jnp.int32, bias_out.shape, 1)
    bias_sums = jnp.zeros(bias_out.shape, jnp.float32)
    own[VALUE].wait()
    for r in range(n):
        b = source_of(r)
        if r > 0:
            wait_in(VALUE, vbuf.at[b], b)
        dprobs = lax.dot_general(
            vbuf[b], g_all, (((1,), (1,)), ((), ())), preferred_element_type=jnp.float32
        )
        dscores = probs[b] * (dprobs - delta)
        half = dscores.astype(jnp.bfloat16)
        ds_half[b] = half
        grad = jnp.dot(half, q_all, preferred_element_type=jnp.float32)
        if r > 0:
            dk_out[b] = (grad * scale).astype(jnp.bfloat16)
            send(back_copy(DKEY, dk_out, dk_ref, b))
        else:
            dk_ref[:, lanes(me)] = (grad * scale).astype(jnp.bfloat16)
        block_sum = jnp.sum(jnp.sum(dscores, axis=0, keepdims=True), axis=1, keepdims=True)
        bias_sums = bias_sums + jnp.where(spot == b, block_sum, 0.0)
    bias_out[...] = bias_sums
    bias_sent = []
    for r in range(1, ndp):
        copy = pltpu.make_async_remote_copy(
            src_ref=bias_out,
            dst_ref=bias_in.at[here],
            send_sem=bias_send.at[r],
            recv_sem=bias_recv.at[here],
            device_id={"dp": lax.rem(here + r, ndp)},
            device_id_type=MESH,
        )
        copy.start()
        bias_sent.append(copy)
    bias_in[here] = bias_sums

    k_all = kbuf[...].reshape(hits, head_dim)
    for r in range(n):
        b = peer_of(r) if r < n - 1 else me
        picked = ds_half[:, :, pl.ds(pl.multiple_of(b * rows, rows), rows)].reshape(hits, rows)
        grad = lax.dot_general(
            picked, k_all, (((0,), (0,)), ((), ())), preferred_element_type=jnp.float32
        )
        if r < n - 1:
            dq_out[b] = (grad * scale).astype(jnp.bfloat16)
            send(back_copy(DQUERY, dq_out, dq_ref, b))
        else:
            dq_ref[:, lanes(me)] = (grad * scale).astype(jnp.bfloat16)

    for r in range(1, ndp):
        other = lax.rem(here + r, ndp)
        pltpu.make_async_remote_copy(
            src_ref=bias_in.at[other],
            dst_ref=bias_in.at[other],
            send_sem=bias_send.at[r],
            recv_sem=bias_recv.at[other],
            device_id={"dp": other},
            device_id_type=MESH,
        ).wait_recv()
    db_ref[...] = jnp.sum(bias_in[...], axis=0)[:, : db_ref.shape[1]]

    for kind, out in ((DVALUE, dv_ref), (DKEY, dk_ref), (DQUERY, dq_ref)):
        for r in range(n - 1):
            peer = peer_of(r)
            wait_in(kind, out.at[:, lanes(peer)], peer)
    for copy in sent + bias_sent:
        copy.wait_send()


def store_kernel(dq_ref, dk_ref, dv_ref, db_ref, dq_hbm, dk_hbm, dv_hbm, db_hbm, sem):
    copies = [
        pltpu.make_async_copy(dq_ref, dq_hbm.at[0], sem.at[0]),
        pltpu.make_async_copy(dk_ref, dk_hbm.at[0], sem.at[1]),
        pltpu.make_async_copy(dv_ref, dv_hbm.at[0], sem.at[2]),
        pltpu.make_async_copy(db_ref, db_hbm, sem.at[3]),
    ]
    for copy in copies:
        copy.start()
    for copy in copies:
        copy.wait()


def on_device(query, key, value, out_ctx, d_out, score_bias, block_list, block_count, hit_count):
    n = lax.axis_size("seq")
    ndp = lax.axis_size("dp")
    _, rows, width = query.shape
    head_dim = width // (score_bias.shape[0] * n)
    assert score_bias.shape[0] == 1 and block_list.shape[1] == n
    hits = n * rows
    padded = -(-n // 128) * 128
    half, full = jnp.bfloat16, jnp.float32
    any_ref = pl.BlockSpec(memory_space=pl.ANY)
    vmem = pl.BlockSpec(memory_space=pltpu.VMEM)
    field = jax.ShapeDtypeStruct(query.shape, query.dtype)
    held = pltpu.VMEM((rows, width), query.dtype)
    grads = pl.pallas_call(
        functools.partial(kernel, n, ndp, head_dim),
        out_shape=(held, held, held, pltpu.VMEM((1, n), full)),
        in_specs=[any_ref] * 9,
        out_specs=(vmem,) * 4,
        scratch_shapes=[
            pltpu.VMEM((n, rows, head_dim), half),
            pltpu.VMEM((n, rows, head_dim), half),
            pltpu.VMEM((n, rows, head_dim), half),
            pltpu.VMEM((n, rows, head_dim), half),
            pltpu.VMEM((n, 1, rows), full),
            pltpu.VMEM((n, 1, rows), full),
            pltpu.VMEM((rows, width), half),
            pltpu.VMEM((rows, width), half),
            pltpu.VMEM((n, rows, hits), full),
            pltpu.VMEM((n, rows, hits), half),
            pltpu.VMEM((n, rows, hits), half),
            pltpu.VMEM((n, rows, head_dim), half),
            pltpu.VMEM((n, rows, head_dim), half),
            pltpu.VMEM((n, rows, head_dim), half),
            pltpu.VMEM((1, padded), full),
            pltpu.VMEM((ndp, 1, padded), full),
            pltpu.SMEM(score_bias.shape, full),
            pltpu.SMEM(block_list.shape, jnp.int32),
            pltpu.SMEM(block_count.shape, jnp.int32),
            pltpu.SMEM(hit_count.shape, jnp.int32),
            pltpu.SemaphoreType.DMA((8, n)),
            pltpu.SemaphoreType.DMA((8, n)),
            pltpu.SemaphoreType.DMA((8,)),
            pltpu.SemaphoreType.DMA((ndp,)),
            pltpu.SemaphoreType.DMA((ndp,)),
            pltpu.SemaphoreType.DMA((4,)),
        ],
        compiler_params=pltpu.CompilerParams(
            collective_id=0, has_side_effects=True, vmem_limit_bytes=60 * 1024 * 1024
        ),
    )(query, key, value, out_ctx, d_out, score_bias, block_list, block_count, hit_count)
    return pl.pallas_call(
        store_kernel,
        out_shape=(field, field, field, jax.ShapeDtypeStruct((1, n), full)),
        in_specs=[any_ref] * 4,
        out_specs=(any_ref,) * 4,
        scratch_shapes=[pltpu.SemaphoreType.DMA((4,))],
    )(*(pltpu.with_memory_space_constraint(x, pltpu.VMEM) for x in grads))


def solution(mesh):
    placed = (
        P("dp", "seq", None),
        P("dp", "seq", None),
        P("dp", "seq", None),
        P("dp", "seq", None),
        P("dp", "seq", None),
        P("seq", None),
        P("seq", None, None),
        P("seq", None),
        P("dp"),
    )
    return jax.shard_map(
        on_device,
        mesh=mesh,
        in_specs=placed,
        out_specs=(
            P("dp", "seq", None),
            P("dp", "seq", None),
            P("dp", "seq", None),
            P("seq", None),
        ),
        check_vma=False,
    )
```

```python
import functools
import math

import jax
import jax.numpy as jnp
from jax import lax
from jax.experimental import pallas as pl
from jax.experimental.pallas import tpu as pltpu
from jax.sharding import PartitionSpec as P

MASKED = -1000000000.0
MESH = pl.DeviceIdType.MESH
KEY, QUERY, GRAD, VALUE, DELTA, DVALUE, DKEY, DQUERY, SHIFT, STATS, BIAS = range(11)


def kernel(
    n,
    ndp,
    head_dim,
    q_hbm,
    k_hbm,
    v_hbm,
    o_hbm,
    g_hbm,
    bias_hbm,
    list_hbm,
    count_hbm,
    hit_hbm,
    dq_ref,
    dk_ref,
    dv_ref,
    db_ref,
    kbuf,
    qbuf,
    gbuf,
    vbuf,
    delta_in,
    delta_out,
    g_own,
    o_own,
    probs,
    probs_half,
    ds_half,
    dv_out,
    dk_out,
    dq_out,
    bias_out,
    bias_in,
    shift_out,
    shift_in,
    stats_out,
    stats_in,
    dq_in,
    btot_out,
    btot_in,
    bias_ref,
    list_ref,
    count_ref,
    hit_ref,
    send_sem,
    recv_sem,
    own_sem,
    bias_send,
    bias_recv,
    table_sem,
):
    me = lax.axis_index("seq")
    here = lax.axis_index("dp")
    rows = q_hbm.shape[1]
    hits = n * rows
    slots = list_ref.shape[2]
    scale = 1.0 / math.sqrt(head_dim)
    above = n - 1 - me
    m = n // 2
    w, u = me % m, me // m
    wide = 2 * head_dim

    def peer_of(r):
        return jnp.where(r < above, n - 1 - r, r - above)

    def near_of(r):
        return u * m + (w + r) % m

    def lanes(z):
        return pl.ds(pl.multiple_of(z % m * wide, wide), wide)

    def slot(kind, z):
        return z if kind in (QUERY, GRAD) else z % m

    load_g = pltpu.make_async_copy(g_hbm.at[0], g_own, own_sem.at[DVALUE])
    load_o = pltpu.make_async_copy(o_hbm.at[0], o_own, own_sem.at[DKEY])
    load_g.start()
    load_o.start()
    tables = [
        pltpu.make_async_copy(src, dst, table_sem.at[i])
        for i, (src, dst) in enumerate(
            ((bias_hbm, bias_ref), (list_hbm, list_ref), (count_hbm, count_ref), (hit_hbm, hit_ref))
        )
    ]
    for copy in tables:
        copy.start()
    sources = {KEY: k_hbm, QUERY: q_hbm, GRAD: g_hbm, VALUE: v_hbm}
    targets = {KEY: kbuf, QUERY: qbuf, GRAD: gbuf, VALUE: vbuf}
    own = {}
    for kind in (KEY, QUERY, GRAD, VALUE):
        own[kind] = pltpu.make_async_copy(
            sources[kind].at[0, :, lanes(me)], targets[kind].at[slot(kind, me)], own_sem.at[kind]
        )
        own[kind].start()

    barrier = pltpu.get_barrier_semaphore()
    for r in range(n - 1):
        pl.semaphore_signal(barrier, inc=1, device_id={"seq": peer_of(r)}, device_id_type=MESH)
    for r in range(1, ndp):
        pl.semaphore_signal(
            barrier, inc=1, device_id={"dp": lax.rem(here + r, ndp)}, device_id_type=MESH
        )
    pl.semaphore_wait(barrier, n - 1 + ndp - 1)

    def out_copy(kind, peer):
        return pltpu.make_async_remote_copy(
            src_ref=sources[kind].at[0, :, lanes(peer)],
            dst_ref=targets[kind].at[slot(kind, me)],
            send_sem=send_sem.at[kind, peer],
            recv_sem=recv_sem.at[kind, me],
            device_id={"seq": peer},
            device_id_type=MESH,
        )

    def wait_in(kind, buf, peer):
        pltpu.make_async_remote_copy(
            src_ref=buf,
            dst_ref=buf,
            send_sem=send_sem.at[kind, peer],
            recv_sem=recv_sem.at[kind, peer],
            device_id={"seq": peer},
            device_id_type=MESH,
        ).wait_recv()

    sent = []

    def send(copy):
        copy.start()
        sent.append(copy)

    def peers(kind):
        if kind in (QUERY, GRAD):
            return [peer_of(r) for r in range(n - 1)]
        return [near_of(r) for r in range(1, m)]

    def push(kind, src, dst, peer):
        return pltpu.make_async_remote_copy(
            src_ref=src,
            dst_ref=dst,
            send_sem=send_sem.at[kind, peer],
            recv_sem=recv_sem.at[kind, me],
            device_id={"seq": peer},
            device_id_type=MESH,
        )

    for kind in (QUERY, KEY):
        for peer in peers(kind):
            send(out_copy(kind, peer))

    for copy in tables:
        copy.wait()
    hit_limit = hit_ref[0]
    lane = lax.broadcasted_iota(jnp.int32, (1, hits), 1)
    within = lax.broadcasted_iota(jnp.int32, (rows, 1), 0)

    def shift_step(b, carry):
        shift = jnp.full((1, hits), MASKED, jnp.float32)
        for qb in range(n):
            used = jnp.int32(0)
            for at in range(slots):
                hit = (list_ref[0, qb, at] == b) & (at < count_ref[0, qb])
                used = jnp.where(hit, jnp.int32(1), used)
            inside = (lane >= qb * rows) & (lane < (qb + 1) * rows)
            shift = jnp.where(inside & (used > 0), bias_ref[0, b], shift)
        shift_out[b // m, b % m] = shift
        return carry

    short = n <= 4
    lax.fori_loop(0, n, shift_step, 0, unroll=short)
    for half in range(2):
        taker = half * m + me // 2

        @pl.when(taker != me)
        def _(half=half, taker=taker):
            push(SHIFT, shift_out.at[half], shift_in.at[me % 2], taker).start()

        @pl.when(taker == me)
        def _(half=half):
            shift_in[me % 2] = shift_out[half]

    load_g.wait()
    load_o.wait()
    for h in range(n):
        cols = slice(h * head_dim, (h + 1) * head_dim)
        product = g_own[:, cols].astype(jnp.float32) * o_own[:, cols].astype(jnp.float32)
        delta_out[h // 2, h % 2] = jnp.sum(product.T, axis=0, keepdims=True)
    for r in range(n - 1):
        peer = peer_of(r)
        send(push(DELTA, delta_out.at[peer % m], delta_in.at[me], peer))
    delta_in[me] = delta_out[w]
    for kind in (GRAD, VALUE):
        for peer in peers(kind):
            send(out_copy(kind, peer))

    def arrive(kind):
        own[kind].wait()
        for peer in peers(kind):
            wait_in(kind, targets[kind].at[slot(kind, peer)], peer)

    arrive(KEY)
    arrive(QUERY)
    for i in range(2):
        head = 2 * w + i

        @pl.when(head != me)
        def _(i=i, head=head):
            wait_in(SHIFT, shift_in.at[i], head)

    def part(field, i):
        return field[..., i * head_dim : (i + 1) * head_dim]

    q_all = qbuf[...].reshape(hits, wide)
    tops = []
    for i in range(2):
        q_head = part(q_all, i)

        def score_step(b, top):
            real = jnp.where((u * m + b) * rows + within < hit_limit, 0.0, MASKED)
            scores = (
                lax.dot_general(
                    part(kbuf[b], i),
                    q_head,
                    (((1,), (1,)), ((), ())),
                    preferred_element_type=jnp.float32,
                )
                * scale
            )
            scores = (scores + shift_in[i, b]) + real
            probs[i, b] = scores
            return jnp.maximum(top, jnp.max(scores, axis=0, keepdims=True))

        top = lax.fori_loop(
            0, m, score_step, jnp.full((1, hits), -3e9, jnp.float32), unroll=short
        )

        def exp_step(b, total):
            raised = jnp.exp(probs[i, b] - top)
            probs[i, b] = raised
            return total + jnp.sum(raised, axis=0, keepdims=True)

        total = lax.fori_loop(0, m, exp_step, jnp.zeros((1, hits), jnp.float32), unroll=short)
        stats_out[i, 0] = top
        stats_out[i, 1] = total
        tops.append((top, total))
    across = (me + m) % n
    send(push(STATS, stats_out, stats_in, across))
    wait_in(STATS, stats_in, across)
    for i in range(2):
        top, total = tops[i]
        best = jnp.maximum(top, stats_in[i, 0])
        mine = jnp.exp(top - best)
        whole = total * mine + stats_in[i, 1] * jnp.exp(stats_in[i, 0] - best)
        factor = jnp.where(lane < hit_limit, mine / whole, 0.0)

        def scale_step(b, carry):
            scaled = probs[i, b] * factor
            probs[i, b] = scaled
            probs_half[i, b] = scaled.astype(jnp.bfloat16)
            return carry

        lax.fori_loop(0, m, scale_step, 0, unroll=short)

    arrive(GRAD)
    g_all = gbuf[...].reshape(hits, wide)
    for r in range(m):
        peer = near_of((r + 1) % m)
        b = peer % m
        for i in range(2):
            grad = jnp.dot(
                probs_half[i, b], part(g_all, i), preferred_element_type=jnp.float32
            )
            dv_out[b, :, i * head_dim : (i + 1) * head_dim] = grad.astype(jnp.bfloat16)
        if r < m - 1:
            send(push(DVALUE, dv_out.at[b], dv_ref.at[:, lanes(me)], peer))
        else:
            dv_ref[:, lanes(me)] = dv_out[b]

    for r in range(n - 1):
        peer = peer_of(r)
        wait_in(DELTA, delta_in.at[peer], peer)
    spot = lax.broadcasted_iota(jnp.int32, (1, bias_out.shape[2]), 1)
    sums = [jnp.zeros(spot.shape, jnp.float32) for _ in range(2)]
    arrive(VALUE)
    for r in range(m):
        peer = near_of((r + 1) % m)
        b = peer % m
        for i in range(2):
            delta = jnp.concatenate([delta_in[z, i] for z in range(n)], axis=1)
            dprobs = lax.dot_general(
                part(vbuf[b], i),
                part(g_all, i),
                (((1,), (1,)), ((), ())),
                preferred_element_type=jnp.float32,
            )
            dscores = probs[i, b] * (dprobs - delta)
            rounded = dscores.astype(jnp.bfloat16)
            ds_half[i, b] = rounded
            grad = jnp.dot(rounded, part(q_all, i), preferred_element_type=jnp.float32)
            dk_out[b, :, i * head_dim : (i + 1) * head_dim] = (grad * scale).astype(jnp.bfloat16)
            block_sum = jnp.sum(jnp.sum(dscores, axis=0, keepdims=True), axis=1, keepdims=True)
            sums[i] = sums[i] + jnp.where(spot == peer, block_sum, 0.0)
        if r < m - 1:
            send(push(DKEY, dk_out.at[b], dk_ref.at[:, lanes(me)], peer))
        else:
            dk_ref[:, lanes(me)] = dk_out[b]

    k_all = kbuf[...].reshape(m * rows, wide)
    for r in range(n):
        b = peer_of(r) if r < n - 1 else me
        for i in range(2):
            picked = ds_half[i, :, :, pl.ds(pl.multiple_of(b * rows, rows), rows)]
            grad = lax.dot_general(
                picked.reshape(m * rows, rows),
                part(k_all, i),
                (((0,), (0,)), ((), ())),
                preferred_element_type=jnp.float32,
            )
            dq_out[b, :, i * head_dim : (i + 1) * head_dim] = (grad * scale).astype(jnp.bfloat16)
        if r < n - 1:
            send(push(DQUERY, dq_out.at[b], dq_in.at[u, :, lanes(me)], b))
        else:
            dq_in[u, :, lanes(me)] = dq_out[b]

    for i in range(2):
        bias_out[i] = sums[i]
        bias_in[here, i] = sums[i]
    bias_sent = []
    for r in range(1, ndp):
        copy = pltpu.make_async_remote_copy(
            src_ref=bias_out,
            dst_ref=bias_in.at[here],
            send_sem=bias_send.at[r],
            recv_sem=bias_recv.at[here],
            device_id={"dp": lax.rem(here + r, ndp)},
            device_id_type=MESH,
        )
        copy.start()
        bias_sent.append(copy)
    for r in range(1, ndp):
        other = lax.rem(here + r, ndp)
        pltpu.make_async_remote_copy(
            src_ref=bias_in.at[other],
            dst_ref=bias_in.at[other],
            send_sem=bias_send.at[r],
            recv_sem=bias_recv.at[other],
            device_id={"dp": other},
            device_id_type=MESH,
        ).wait_recv()
    btot_out[...] = jnp.sum(bias_in[...], axis=0)
    for i in range(2):
        head = 2 * w + i

        @pl.when(head != me)
        def _(i=i, head=head):
            push(BIAS, btot_out.at[i], btot_in.at[u], head).start()

        @pl.when(head == me)
        def _(i=i):
            btot_in[u] = btot_out[i]

    for kind, out in ((DVALUE, dv_ref), (DKEY, dk_ref)):
        for peer in peers(kind):
            wait_in(kind, out.at[:, lanes(peer)], peer)
    for half in range(2):
        taker = half * m + me // 2

        @pl.when(taker != me)
        def _(half=half, taker=taker):
            push(SHIFT, shift_out.at[half], shift_in.at[me % 2], taker).wait_send()
            wait_in(BIAS, btot_in.at[half], taker)

    for i in range(2):
        head = 2 * w + i

        @pl.when(head != me)
        def _(i=i, head=head):
            push(BIAS, btot_out.at[i], btot_in.at[u], head).wait_send()

    db_ref[...] = (btot_in[0] + btot_in[1])[:, : db_ref.shape[1]]
    for r in range(n - 1):
        peer = peer_of(r)
        wait_in(DQUERY, dq_in.at[peer // m, :, lanes(peer)], peer)
    dq_ref[...] = (dq_in[0].astype(jnp.float32) + dq_in[1].astype(jnp.float32)).astype(
        jnp.bfloat16
    )
    for copy in sent + bias_sent:
        copy.wait_send()


def store_kernel(dq_ref, dk_ref, dv_ref, db_ref, dq_hbm, dk_hbm, dv_hbm, db_hbm, sem):
    copies = [
        pltpu.make_async_copy(dq_ref, dq_hbm.at[0], sem.at[0]),
        pltpu.make_async_copy(dk_ref, dk_hbm.at[0], sem.at[1]),
        pltpu.make_async_copy(dv_ref, dv_hbm.at[0], sem.at[2]),
        pltpu.make_async_copy(db_ref, db_hbm, sem.at[3]),
    ]
    for copy in copies:
        copy.start()
    for copy in copies:
        copy.wait()


def on_device(query, key, value, out_ctx, d_out, score_bias, block_list, block_count, hit_count):
    n = lax.axis_size("seq")
    ndp = lax.axis_size("dp")
    _, rows, width = query.shape
    head_dim = width // (score_bias.shape[0] * n)
    assert score_bias.shape[0] == 1 and block_list.shape[1] == n
    m, wide = n // 2, 2 * head_dim
    hits = n * rows
    padded = -(-n // 128) * 128
    half, full = jnp.bfloat16, jnp.float32
    any_ref = pl.BlockSpec(memory_space=pl.ANY)
    vmem = pl.BlockSpec(memory_space=pltpu.VMEM)
    field = jax.ShapeDtypeStruct(query.shape, query.dtype)
    held = pltpu.VMEM((rows, width), query.dtype)
    grads = pl.pallas_call(
        functools.partial(kernel, n, ndp, head_dim),
        out_shape=(held, held, held, pltpu.VMEM((1, n), full)),
        in_specs=[any_ref] * 9,
        out_specs=(vmem,) * 4,
        scratch_shapes=[
            pltpu.VMEM((m, rows, wide), half),
            pltpu.VMEM((n, rows, wide), half),
            pltpu.VMEM((n, rows, wide), half),
            pltpu.VMEM((m, rows, wide), half),
            pltpu.VMEM((n, 2, 1, rows), full),
            pltpu.VMEM((m, 2, 1, rows), full),
            pltpu.VMEM((rows, width), half),
            pltpu.VMEM((rows, width), half),
            pltpu.VMEM((2, m, rows, hits), full),
            pltpu.VMEM((2, m, rows, hits), half),
            pltpu.VMEM((2, m, rows, hits), half),
            pltpu.VMEM((m, rows, wide), half),
            pltpu.VMEM((m, rows, wide), half),
            pltpu.VMEM((n, rows, wide), half),
            pltpu.VMEM((2, 1, padded), full),
            pltpu.VMEM((ndp, 2, 1, padded), full),
            pltpu.VMEM((2, m, 1, hits), full),
            pltpu.VMEM((2, m, 1, hits), full),
            pltpu.VMEM((2, 2, 1, hits), full),
            pltpu.VMEM((2, 2, 1, hits), full),
            pltpu.VMEM((2, rows, width), half),
            pltpu.VMEM((2, 1, padded), full),
            pltpu.VMEM((2, 1, padded), full),
            pltpu.SMEM(score_bias.shape, full),
            pltpu.SMEM(block_list.shape, jnp.int32),
            pltpu.SMEM(block_count.shape, jnp.int32),
            pltpu.SMEM(hit_count.shape, jnp.int32),
            pltpu.SemaphoreType.DMA((11, n)),
            pltpu.SemaphoreType.DMA((11, n)),
            pltpu.SemaphoreType.DMA((8,)),
            pltpu.SemaphoreType.DMA((ndp,)),
            pltpu.SemaphoreType.DMA((ndp,)),
            pltpu.SemaphoreType.DMA((4,)),
        ],
        compiler_params=pltpu.CompilerParams(
            collective_id=0, has_side_effects=True, vmem_limit_bytes=60 * 1024 * 1024
        ),
    )(query, key, value, out_ctx, d_out, score_bias, block_list, block_count, hit_count)
    return pl.pallas_call(
        store_kernel,
        out_shape=(field, field, field, jax.ShapeDtypeStruct((1, n), full)),
        in_specs=[any_ref] * 4,
        out_specs=(any_ref,) * 4,
        scratch_shapes=[pltpu.SemaphoreType.DMA((4,))],
    )(*(pltpu.with_memory_space_constraint(x, pltpu.VMEM) for x in grads))


def solution(mesh):
    placed = (
        P("dp", "seq", None),
        P("dp", "seq", None),
        P("dp", "seq", None),
        P("dp", "seq", None),
        P("dp", "seq", None),
        P("seq", None),
        P("seq", None, None),
        P("seq", None),
        P("dp"),
    )
    return jax.shard_map(
        on_device,
        mesh=mesh,
        in_specs=placed,
        out_specs=(
            P("dp", "seq", None),
            P("dp", "seq", None),
            P("dp", "seq", None),
            P("seq", None),
        ),
        check_vma=False,
    )
```
